32 devices in a mesh: groups: 2 (over y), tile: 4 (over z), tm: 4 (over x, core).
Axes of the slice: x: 2, y: 2, z: 4, core: 2. Of those that a mesh axis runs over, the one named last changes fastest.
Arguments:
- hidden: bfloat16 [8, 16, 3072], P(('groups', 'tm'), 'tile'), parts along dimension 0, may hold values from -12 to 12
- modulation: float32 [4, 3072], P('groups'), parts along dimension 0, may hold values from -2.5 to 2.5
- proj_weight: bfloat16 [3072, 64], replicated, may hold values from -0.109375 to 0.109375
- conv_in_weight: bfloat16 [3, 3, 3, 16, 256], replicated, may hold values from -0.3125 to 0.3125
- up_weight: bfloat16 [3, 3, 3, 256, 256], replicated, may hold values from -0.15625 to 0.15625
Outputs:
- decoded: bfloat16 [8, 16, 16, 256], P(('groups', 'tm'), None, 'tile'), parts along dimension 0
The draws below stay inside these ranges and needn't reach their ends.
There are 2 independent parts, one for each index of `groups`. The reference program is written for one: setup_inputs(seed, part) draws one part's arguments, and reference() takes and returns one part's arrays. A program takes and returns all parts, laid end to end along the dimension named above; an argument that names none is the same for every part. Nothing has to cross between parts.
All inputs are finite; a program needn't handle non-finite values.
Results may differ from the reference program's by a relative error of at most 0.0065.
Values may be sent and summed in bfloat16 or wider, within the bound.
A program may use at most 64 MiB of HBM per device.

```python
import math
import jax
import jax.numpy as jnp
from jax import lax

D = 3072
LAT_CH = 16
CH = 256
FRAMES = 4
TOK_ROWS = 4
TOK_COLS = 4


def draw_hidden(key, part):
    shape_all = (FRAMES, TOK_ROWS * TOK_COLS, D)
    key_base, key_cols, key_rows = jax.random.split(key, 3)
    col_scale = jnp.exp(jax.random.uniform(key_cols, (D,), jnp.float32, math.log(0.3), math.log(3.0)))
    row_scale = jnp.exp(jax.random.uniform(key_rows, (FRAMES, TOK_ROWS * TOK_COLS, 1), jnp.float32, math.log(0.5), math.log(2.0)))
    values = jax.random.normal(key_base, shape_all, jnp.float32) * col_scale * row_scale
    return jnp.clip(values, -12.0, 12.0).astype(jnp.bfloat16)


def scatter_about(rng, extent, deviation, bound, kind=jnp.bfloat16):
    array = jax.random.normal(rng, extent, jnp.float32) * deviation
    return jnp.minimum(jnp.maximum(array, -bound), bound).astype(kind)


def setup_inputs(seed: int = 0, part: int = 0) -> dict:
    splits = jax.random.split(jax.random.key(seed), 6)
    own_keys = jax.random.split(jax.random.fold_in(splits[5], part), 6)
    return {
        "hidden": draw_hidden(jax.random.fold_in(jax.random.fold_in(splits[5], part), 71), part),
        "modulation": scatter_about(own_keys[1], (2, D), 0.5, 2.5, jnp.float32),
        "proj_weight": scatter_about(splits[2], (D, 4 * LAT_CH), D ** -0.5, 0.109375),
        "conv_in_weight": scatter_about(splits[3], (3, 3, 3, LAT_CH, CH), (27 * LAT_CH) ** -0.5, 0.3125),
        "up_weight": scatter_about(splits[4], (3, 3, 3, CH, CH), (27 * CH // 4) ** -0.5, 0.15625),
    }


def unpatch(patches, lat_ch):
    frames_n, rows_n, cols_n, _ = patches.shape
    split_up = patches.reshape(frames_n, rows_n, cols_n, 2, 2, lat_ch)
    return split_up.transpose(0, 1, 3, 2, 4, 5).reshape(frames_n, 2 * rows_n, 2 * cols_n, lat_ch)

def causal_conv(field, kernel):
    first_frame = field[:1]
    padded = jnp.concatenate([first_frame, first_frame, field], axis=0)
    padded = jnp.pad(padded, ((0, 0), (1, 1), (1, 1), (0, 0)))
    result = lax.conv_general_dilated(padded[None], kernel, (1, 1, 1), 'VALID', dimension_numbers=('NDHWC', 'DHWIO', 'NDHWC'), preferred_element_type=jnp.float32)
    return result[0]

def reference(hidden, modulation, proj_weight, conv_in_weight, up_weight):
    values = hidden.astype(jnp.float32)
    row_mean = lax.optimization_barrier(jnp.mean(values, axis=-1, keepdims=True))
    centred = values - row_mean
    row_var = lax.optimization_barrier(jnp.mean(centred * centred, axis=-1, keepdims=True))
    normed = centred * lax.rsqrt(row_var + 1e-06)
    modulated = (normed * (1.0 + modulation[1]) + modulation[0]).astype(jnp.bfloat16)
    flat_rows = modulated.reshape(-1, modulated.shape[-1])
    projected = jnp.dot(flat_rows, proj_weight, preferred_element_type=jnp.float32).astype(jnp.bfloat16)
    patches = projected.reshape(FRAMES, TOK_ROWS, TOK_COLS, 4 * LAT_CH)
    latent = unpatch(patches, LAT_CH)
    features = jax.nn.silu(causal_conv(latent, conv_in_weight)).astype(jnp.bfloat16)
    doubled = jnp.repeat(jnp.repeat(features, 2, axis=1), 2, axis=2)
    return causal_conv(doubled, up_weight).astype(jnp.bfloat16)
```

```python
import functools

import jax
import jax.numpy as jnp
from jax import lax
from jax.experimental import pallas as pl
from jax.experimental.pallas import tpu as pltpu
from jax.sharding import PartitionSpec as P

REACH = 5
EDGE = 8
UP_CHUNKS = 9
MESH = pl.DeviceIdType.MESH


def fused_kernel(
    n_tile,
    n_tm,
    hidden_hbm,
    mod_hbm,
    proj_hbm,
    cin_hbm,
    up_hbm,
    out_ref,
    hid,
    mod,
    proj,
    cin,
    upw,
    pad_p,
    outbox,
    inbox,
    lat,
    feat,
    pairs,
    joined,
    load_sem,
    up_sem,
    send_sem,
    recv_sem,
    own_sem,
):
    tile = lax.axis_index("tile")
    frame = lax.axis_index("tm")
    rows = 2 * n_tile
    first = jnp.maximum(frame - (REACH - 1), 0)
    after = jnp.minimum(frame + REACH, n_tm)

    barrier = pltpu.get_barrier_semaphore()

    def greet_frame(source, _):
        def greet(column, _):
            @pl.when(jnp.logical_or(source != frame, column != tile))
            def _():
                pl.semaphore_signal(
                    barrier,
                    inc=1,
                    device_id={"tile": column, "tm": source},
                    device_id_type=MESH,
                )

            return 0

        return lax.fori_loop(0, n_tile, greet, 0)

    lax.fori_loop(first, frame + 1, greet_frame, 0)

    loads = [
        pltpu.make_async_copy(hidden_hbm.at[0], hid, load_sem.at[0]),
        pltpu.make_async_copy(mod_hbm, mod, load_sem.at[1]),
        pltpu.make_async_copy(proj_hbm, proj, load_sem.at[2]),
    ]
    load_cin = pltpu.make_async_copy(cin_hbm, cin.at[:, pl.ds(0, 48), :], load_sem.at[3])
    per_chunk = 27 // UP_CHUNKS
    load_up = [
        pltpu.make_async_copy(
            up_hbm.at[pl.ds(n * per_chunk, per_chunk)],
            upw.at[pl.ds(n * per_chunk, per_chunk)],
            up_sem.at[n],
        )
        for n in range(UP_CHUNKS)
    ]
    for copy in loads + [load_cin] + load_up:
        copy.start()

    cin[:, 48:, :] = jnp.zeros((9, 80, 256), jnp.bfloat16)
    pad_p[...] = jnp.zeros_like(pad_p)
    for k in range(4):
        for slot in range(REACH):
            lat[k, slot, 0:EDGE, :] = jnp.zeros((EDGE, 128), jnp.float32)
            lat[k, slot, EDGE + rows :, :] = jnp.zeros((EDGE, 128), jnp.float32)
        for t in range(3):
            feat[k, t, 0:EDGE, :] = jnp.zeros((EDGE, 256), jnp.float32)
            feat[k, t, EDGE + rows :, :] = jnp.zeros((EDGE, 256), jnp.float32)

    loads[0].wait()
    values = hid[...].astype(jnp.float32)
    width = values.shape[-1]
    mean = jnp.sum(values, axis=-1, keepdims=True) * (1.0 / width)
    centred = values - mean
    var = jnp.sum(centred * centred, axis=-1, keepdims=True) * (1.0 / width)
    normed = centred * lax.rsqrt(var + 1e-06)
    loads[1].wait()
    modulated = (normed * (1.0 + mod[1:2, :]) + mod[0:1, :]).astype(jnp.bfloat16)
    loads[2].wait()
    patches = lax.dot_general(
        modulated, proj[...], (((1,), (1,)), ((), ())), preferred_element_type=jnp.float32
    )
    pad_p[0:n_tile, 0:64] = patches.astype(jnp.bfloat16).astype(jnp.float32)

    padded = pad_p[...]
    height = padded.shape[0]
    lanes = lax.broadcasted_iota(jnp.int32, padded.shape, 1)
    for i in range(2):
        own = padded if i == 0 else pltpu.roll(padded, 96, 1)
        own = jnp.where(lanes < 32, own, 0.0)
        window = (
            pltpu.roll(own, 1, 0)
            + pltpu.roll(own, 32, 1)
            + pltpu.roll(pltpu.roll(own, height - 1, 0), 64, 1)
        )
        for column in range(n_tile):
            outbox[column, i : i + 1, :] = window[column : column + 1, :]

    own_copy = pltpu.make_async_copy(outbox.at[tile], inbox.at[0, tile], own_sem)
    own_copy.start()
    pl.semaphore_wait(barrier, (after - frame) * n_tile - 1)

    for d in range(REACH):

        @pl.when(frame + d < n_tm)
        def _(d=d):
            def send(step, _):
                column = lax.rem(tile + step, n_tile)
                pltpu.make_async_remote_copy(
                    src_ref=outbox.at[column],
                    dst_ref=inbox.at[d, tile],
                    send_sem=send_sem.at[d],
                    recv_sem=recv_sem.at[d],
                    device_id={"tile": column, "tm": frame + d},
                    device_id_type=MESH,
                ).start()
                return 0

            lax.fori_loop(1 if d == 0 else 0, n_tile, send, 0)

    own_copy.wait()
    for d in range(REACH):
        count = n_tile - 1 if d == 0 else n_tile

        @pl.when(frame - d >= 0)
        def _(d=d, count=count):
            arrived = inbox.at[d, pl.ds(0, count)]
            pltpu.make_async_copy(arrived, arrived, recv_sem.at[d]).wait()

    for slot in range(REACH):
        distance = jnp.minimum(REACH - 1 - slot, frame)
        for r in range(n_tile):
            lat[0, slot, EDGE + 2 * r : EDGE + 2 * r + 2, :] = inbox[distance, r]
        field = lat[0, slot, EDGE : EDGE + rows, :]
        for k in range(1, 4):
            lat[k, slot, EDGE : EDGE + rows, :] = pltpu.roll(field, 128 - 16 * k, 1)

    load_cin.wait()
    taps = []
    for a in range(3):
        for b in range(3):
            start = EDGE - 1 + b
            taps.append(
                jnp.concatenate(
                    [
                        lat[k, t + a, start : start + rows, :]
                        for k in range(4)
                        for t in range(3)
                    ],
                    axis=0,
                ).astype(jnp.bfloat16)
            )
    summed = jnp.dot(
        jnp.concatenate(taps, axis=1),
        cin[...].reshape(9 * 128, 256),
        preferred_element_type=jnp.float32,
    )
    features = (summed / (1.0 + jnp.exp(-summed))).astype(jnp.bfloat16).astype(jnp.float32)
    for k in range(4):
        column = 2 * tile - 1 + k
        inside = jnp.logical_and(column >= 0, column < 2 * n_tile)
        for t in range(3):
            block = features[(3 * k + t) * rows : (3 * k + t + 1) * rows]
            if k in (0, 3):
                block = jnp.where(inside, block, 0.0)
            feat[k, t, EDGE : EDGE + rows, :] = block

    for tap_y in range(3):
        for t in range(3):
            for k in range(4):
                pairs[tap_y, t, k] = jnp.concatenate(
                    [
                        feat[k, t, EDGE + (p + tap_y - 1) // 2 : EDGE + (p + tap_y - 1) // 2 + rows, :]
                        for p in range(2)
                    ],
                    axis=0,
                ).astype(jnp.bfloat16)

    total = None
    for t in range(3):
        for tap_y in range(3):
            for tap_x in range(3):
                tap = (3 * t + tap_y) * 3 + tap_x
                if tap % per_chunk == 0:
                    load_up[tap // per_chunk].wait()
                left = jnp.concatenate(
                    [pairs[tap_y, t, (x + tap_x - 1) // 2 + 1] for x in range(4)], axis=0
                )
                part = jnp.dot(left, upw[tap], preferred_element_type=jnp.float32)
                total = part if total is None else total + part

    for x in range(4):
        for p in range(2):
            at = (2 * x + p) * rows
            for half in range(2):
                joined[half, pl.ds(4 * p + x, rows, stride=8), :] = total[
                    at : at + rows, 128 * half : 128 * (half + 1)
                ]
    for row in range(2 * rows):
        for half in range(2):
            out_ref[0, row, :, 128 * half : 128 * (half + 1)] = joined[
                half, 4 * row : 4 * row + 4, :
            ].astype(jnp.bfloat16)

    for d in range(REACH):
        count = n_tile - 1 if d == 0 else n_tile

        @pl.when(frame + d < n_tm)
        def _(d=d, count=count):
            left = outbox.at[pl.ds(0, count)]
            pltpu.make_async_copy(left, left, send_sem.at[d]).wait()


def on_device(n_tile, n_tm, hidden, modulation, proj_weight, conv_in_weight, up_weight):
    frames_dev, tokens, width = hidden.shape
    lat_ch, channels = conv_in_weight.shape[3:]
    assert frames_dev == 1 and tokens == n_tile and lat_ch == 16 and channels == 256
    rows = 2 * n_tile
    field = rows + 2 * EDGE
    hbm = pl.BlockSpec(memory_space=pltpu.HBM)
    return pl.pallas_call(
        functools.partial(fused_kernel, n_tile, n_tm),
        out_shape=jax.ShapeDtypeStruct((1, 2 * rows, 4, channels), jnp.bfloat16),
        in_specs=[hbm] * 5,
        out_specs=pl.BlockSpec(memory_space=pltpu.VMEM),
        scratch_shapes=[
            pltpu.VMEM((tokens, width), jnp.bfloat16),
            pltpu.VMEM((2, width), jnp.float32),
            pltpu.VMEM((4 * lat_ch, width), jnp.bfloat16),
            pltpu.VMEM((9, 128, channels), jnp.bfloat16),
            pltpu.VMEM((27, channels, channels), jnp.bfloat16),
            pltpu.VMEM(((tokens // 8 + 1) * 8, 128), jnp.float32),
            pltpu.VMEM((n_tile, 2, 128), jnp.float32),
            pltpu.VMEM((REACH, n_tile, 2, 128), jnp.float32),
            pltpu.VMEM((4, REACH, field, 128), jnp.float32),
            pltpu.VMEM((4, 3, field, channels), jnp.float32),
            pltpu.VMEM((3, 3, 4, 2 * rows, channels), jnp.bfloat16),
            pltpu.VMEM((2, 8 * rows, 128), jnp.float32),
            pltpu.SemaphoreType.DMA((4,)),
            pltpu.SemaphoreType.DMA((UP_CHUNKS,)),
            pltpu.SemaphoreType.DMA((REACH,)),
            pltpu.SemaphoreType.DMA((REACH,)),
            pltpu.SemaphoreType.DMA,
        ],
        compiler_params=pltpu.CompilerParams(
            collective_id=0, has_side_effects=True
        ),
    )(
        hidden,
        modulation,
        proj_weight.T,
        conv_in_weight.reshape(9, 48, channels),
        up_weight.reshape(27, channels, channels),
    )


def solution(mesh):
    in_specs = (P(("groups", "tm"), "tile", None), P("groups", None), P(), P(), P())
    out_specs = P(("groups", "tm"), None, "tile", None)
    body = functools.partial(on_device, mesh.shape["tile"], mesh.shape["tm"])
    return jax.shard_map(
        body, mesh=mesh, in_specs=in_specs, out_specs=out_specs, check_vma=False
    )
```

```python
import functools

import jax
import jax.numpy as jnp
from jax import lax
from jax.experimental import pallas as pl
from jax.experimental.pallas import tpu as pltpu
from jax.sharding import PartitionSpec as P

REACH = 5
EDGE = 8
UP_CHUNKS = 9
MESH = pl.DeviceIdType.MESH


def fused_kernel(
    n_tile,
    n_tm,
    hidden_hbm,
    mod_hbm,
    proj_hbm,
    cin_hbm,
    up_hbm,
    out_ref,
    hid,
    mod,
    proj,
    cin,
    upw,
    pad_p,
    outbox,
    inbox,
    lat,
    feat,
    pairs,
    joined,
    load_sem,
    up_sem,
    send_sem,
    recv_sem,
    own_sem,
):
    tile = lax.axis_index("tile")
    frame = lax.axis_index("tm")
    rows = 2 * n_tile
    first = jnp.maximum(frame - (REACH - 1), 0)
    after = jnp.minimum(frame + REACH, n_tm)

    barrier = pltpu.get_barrier_semaphore()

    def greet_frame(source, _):
        def greet(column, _):
            @pl.when(jnp.logical_or(source != frame, column != tile))
            def _():
                pl.semaphore_signal(
                    barrier,
                    inc=1,
                    device_id={"tile": column, "tm": source},
                    device_id_type=MESH,
                )

            return 0

        return lax.fori_loop(0, n_tile, greet, 0)

    lax.fori_loop(first, frame + 1, greet_frame, 0)

    loads = [
        pltpu.make_async_copy(hidden_hbm.at[0], hid, load_sem.at[0]),
        pltpu.make_async_copy(mod_hbm, mod, load_sem.at[1]),
        pltpu.make_async_copy(proj_hbm, proj, load_sem.at[2]),
    ]
    load_cin = pltpu.make_async_copy(cin_hbm, cin.at[:, pl.ds(0, 48), :], load_sem.at[3])
    per_chunk = 27 // UP_CHUNKS
    load_up = [
        pltpu.make_async_copy(
            up_hbm.at[pl.ds(n * per_chunk, per_chunk)],
            upw.at[pl.ds(n * per_chunk, per_chunk)],
            up_sem.at[n],
        )
        for n in range(UP_CHUNKS)
    ]
    for copy in loads + [load_cin] + load_up:
        copy.start()

    cin[:, 48:, :] = jnp.zeros((9, 80, 256), jnp.bfloat16)
    pad_p[...] = jnp.zeros_like(pad_p)
    for k in range(4):
        for slot in range(REACH):
            lat[k, slot, 0:EDGE, :] = jnp.zeros((EDGE, 128), jnp.float32)
            lat[k, slot, EDGE + rows :, :] = jnp.zeros((EDGE, 128), jnp.float32)
        for t in range(3):
            feat[k, t, 0:EDGE, :] = jnp.zeros((EDGE, 256), jnp.float32)
            feat[k, t, EDGE + rows :, :] = jnp.zeros((EDGE, 256), jnp.float32)

    loads[0].wait()
    values = hid[...].astype(jnp.float32)
    width = values.shape[-1]
    mean = jnp.sum(values, axis=-1, keepdims=True) * (1.0 / width)
    centred = values - mean
    var = jnp.sum(centred * centred, axis=-1, keepdims=True) * (1.0 / width)
    normed = centred * lax.rsqrt(var + 1e-06)
    loads[1].wait()
    modulated = (normed * (1.0 + mod[1:2, :]) + mod[0:1, :]).astype(jnp.bfloat16)
    loads[2].wait()
    patches = lax.dot_general(
        modulated, proj[...], (((1,), (1,)), ((), ())), preferred_element_type=jnp.float32
    )
    pad_p[0:n_tile, 0:64] = patches.astype(jnp.bfloat16).astype(jnp.float32)

    padded = pad_p[...]
    height = padded.shape[0]
    lanes = lax.broadcasted_iota(jnp.int32, padded.shape, 1)
    for i in range(2):
        own = padded if i == 0 else pltpu.roll(padded, 96, 1)
        own = jnp.where(lanes < 32, own, 0.0)
        window = (
            pltpu.roll(own, 1, 0)
            + pltpu.roll(own, 32, 1)
            + pltpu.roll(pltpu.roll(own, height - 1, 0), 64, 1)
        )
        for column in range(n_tile):
            outbox[column, i : i + 1, :] = window[column : column + 1, :]

    own_copy = pltpu.make_async_copy(outbox.at[tile], inbox.at[0, tile], own_sem)
    own_copy.start()
    pl.semaphore_wait(barrier, (after - frame) * n_tile - 1)

    for d in range(REACH):

        @pl.when(frame + d < n_tm)
        def _(d=d):
            def send(step, _):
                column = lax.rem(tile + step, n_tile)
                pltpu.make_async_remote_copy(
                    src_ref=outbox.at[column],
                    dst_ref=inbox.at[d, tile],
                    send_sem=send_sem.at[d],
                    recv_sem=recv_sem.at[d],
                    device_id={"tile": column, "tm": frame + d},
                    device_id_type=MESH,
                ).start()
                return 0

            lax.fori_loop(1 if d == 0 else 0, n_tile, send, 0)

    own_copy.wait()
    for d in range(REACH):
        count = n_tile - 1 if d == 0 else n_tile

        @pl.when(frame - d >= 0)
        def _(d=d, count=count):
            arrived = inbox.at[d, pl.ds(0, count)]
            pltpu.make_async_copy(arrived, arrived, recv_sem.at[d]).wait()

    for slot in range(REACH):
        distance = jnp.minimum(REACH - 1 - slot, frame)
        for r in range(n_tile):
            lat[0, slot, EDGE + 2 * r : EDGE + 2 * r + 2, :] = inbox[distance, r]
        field = lat[0, slot, EDGE : EDGE + rows, :]
        for k in range(1, 4):
            lat[k, slot, EDGE : EDGE + rows, :] = pltpu.roll(field, 128 - 16 * k, 1)

    load_cin.wait()
    taps = []
    for a in range(3):
        for b in range(3):
            start = EDGE - 1 + b
            taps.append(
                jnp.concatenate(
                    [
                        lat[k, t + a, start : start + rows, :]
                        for k in range(4)
                        for t in range(3)
                    ],
                    axis=0,
                ).astype(jnp.bfloat16)
            )
    summed = jnp.dot(
        jnp.concatenate(taps, axis=1),
        cin[...].reshape(9 * 128, 256),
        preferred_element_type=jnp.float32,
    )
    features = (summed / (1.0 + jnp.exp(-summed))).astype(jnp.bfloat16).astype(jnp.float32)
    for k in range(4):
        column = 2 * tile - 1 + k
        inside = jnp.logical_and(column >= 0, column < 2 * n_tile)
        for t in range(3):
            block = features[(3 * k + t) * rows : (3 * k + t + 1) * rows]
            if k in (0, 3):
                block = jnp.where(inside, block, 0.0)
            feat[k, t, EDGE : EDGE + rows, :] = block

    for tap_y in range(3):
        for t in range(3):
            for k in range(4):
                pairs[tap_y, t, k] = jnp.concatenate(
                    [
                        feat[k, t, EDGE + (p + tap_y - 1) // 2 : EDGE + (p + tap_y - 1) // 2 + rows, :]
                        for p in range(2)
                    ],
                    axis=0,
                ).astype(jnp.bfloat16)

    total = None
    for t in range(3):
        for tap_y in range(3):
            for tap_x in range(3):
                tap = (3 * t + tap_y) * 3 + tap_x
                if tap % per_chunk == 0:
                    load_up[tap // per_chunk].wait()
                left = jnp.concatenate(
                    [pairs[tap_y, t, (x + tap_x - 1) // 2 + 1] for x in range(4)], axis=0
                )
                part = jnp.dot(left, upw[tap], preferred_element_type=jnp.float32)
                total = part if total is None else total + part

    for x in range(4):
        for p in range(2):
            at = (2 * x + p) * rows
            for half in range(2):
                joined[half, pl.ds(4 * p + x, rows, stride=8), :] = total[
                    at : at + rows, 128 * half : 128 * (half + 1)
                ]
    for row in range(2 * rows):
        for half in range(2):
            out_ref[0, row, :, 128 * half : 128 * (half + 1)] = joined[
                half, 4 * row : 4 * row + 4, :
            ].astype(jnp.bfloat16)

    for d in range(REACH):
        count = n_tile - 1 if d == 0 else n_tile

        @pl.when(frame + d < n_tm)
        def _(d=d, count=count):
            left = outbox.at[pl.ds(0, count)]
            pltpu.make_async_copy(left, left, send_sem.at[d]).wait()


def on_device(n_tile, n_tm, hidden, modulation, proj_weight, conv_in_weight, up_weight):
    frames_dev, tokens, width = hidden.shape
    lat_ch, channels = conv_in_weight.shape[3:]
    assert frames_dev == 1 and tokens == n_tile and lat_ch == 16 and channels == 256
    rows = 2 * n_tile
    field = rows + 2 * EDGE
    hbm = pl.BlockSpec(memory_space=pltpu.HBM)
    return pl.pallas_call(
        functools.partial(fused_kernel, n_tile, n_tm),
        out_shape=pltpu.VMEM((1, 2 * rows, 4, channels), jnp.bfloat16),
        in_specs=[hbm] * 5,
        out_specs=pl.BlockSpec(memory_space=pltpu.VMEM),
        scratch_shapes=[
            pltpu.VMEM((tokens, width), jnp.bfloat16),
            pltpu.VMEM((2, width), jnp.float32),
            pltpu.VMEM((4 * lat_ch, width), jnp.bfloat16),
            pltpu.VMEM((9, 128, channels), jnp.bfloat16),
            pltpu.VMEM((27, channels, channels), jnp.bfloat16),
            pltpu.VMEM(((tokens // 8 + 1) * 8, 128), jnp.float32),
            pltpu.VMEM((n_tile, 2, 128), jnp.float32),
            pltpu.VMEM((REACH, n_tile, 2, 128), jnp.float32),
            pltpu.VMEM((4, REACH, field, 128), jnp.float32),
            pltpu.VMEM((4, 3, field, channels), jnp.float32),
            pltpu.VMEM((3, 3, 4, 2 * rows, channels), jnp.bfloat16),
            pltpu.VMEM((2, 8 * rows, 128), jnp.float32),
            pltpu.SemaphoreType.DMA((4,)),
            pltpu.SemaphoreType.DMA((UP_CHUNKS,)),
            pltpu.SemaphoreType.DMA((REACH,)),
            pltpu.SemaphoreType.DMA((REACH,)),
            pltpu.SemaphoreType.DMA,
        ],
        compiler_params=pltpu.CompilerParams(
            collective_id=0, has_side_effects=True
        ),
    )(
        hidden,
        modulation,
        proj_weight.T,
        conv_in_weight.reshape(9, 48, channels),
        up_weight.reshape(27, channels, channels),
    )


def solution(mesh):
    in_specs = (P(("groups", "tm"), "tile", None), P("groups", None), P(), P(), P())
    out_specs = P(("groups", "tm"), None, "tile", None)
    body = functools.partial(on_device, mesh.shape["tile"], mesh.shape["tm"])
    return jax.shard_map(
        body, mesh=mesh, in_specs=in_specs, out_specs=out_specs, check_vma=False
    )
```

```python
import functools

import jax
import jax.numpy as jnp
from jax import lax
from jax.experimental import pallas as pl
from jax.experimental.pallas import tpu as pltpu
from jax.sharding import PartitionSpec as P

REACH = 5
EDGE = 8
UP_CHUNKS = 3
MESH = pl.DeviceIdType.MESH


def fused_kernel(
    n_tile,
    n_tm,
    hidden_hbm,
    mod_hbm,
    proj_hbm,
    cin_hbm,
    up_hbm,
    out_ref,
    hid,
    mod,
    proj,
    cin,
    upw,
    pad_p,
    outbox,
    inbox,
    lat,
    feat,
    pairs,
    joined,
    load_sem,
    up_sem,
    send_sem,
    recv_sem,
    own_sem,
):
    tile = lax.axis_index("tile")
    frame = lax.axis_index("tm")
    rows = 2 * n_tile
    first = jnp.maximum(frame - (REACH - 1), 0)
    after = jnp.minimum(frame + REACH, n_tm)

    barrier = pltpu.get_barrier_semaphore()

    def greet_frame(source, _):
        def greet(column, _):
            @pl.when(jnp.logical_or(source != frame, column != tile))
            def _():
                pl.semaphore_signal(
                    barrier,
                    inc=1,
                    device_id={"tile": column, "tm": source},
                    device_id_type=MESH,
                )

            return 0

        return lax.fori_loop(0, n_tile, greet, 0)

    lax.fori_loop(first, frame + 1, greet_frame, 0)

    loads = [
        pltpu.make_async_copy(hidden_hbm.at[0], hid, load_sem.at[0]),
        pltpu.make_async_copy(mod_hbm, mod, load_sem.at[1]),
        pltpu.make_async_copy(proj_hbm, proj, load_sem.at[2]),
    ]
    load_cin = pltpu.make_async_copy(cin_hbm, cin.at[:, pl.ds(0, 48), :], load_sem.at[3])
    per_chunk = 27 // UP_CHUNKS
    load_up = [
        pltpu.make_async_copy(
            up_hbm.at[pl.ds(n * per_chunk, per_chunk)],
            upw.at[pl.ds(n * per_chunk, per_chunk)],
            up_sem.at[n],
        )
        for n in range(UP_CHUNKS)
    ]
    for copy in loads:
        copy.start()

    cin[:, 48:, :] = jnp.zeros((9, 80, 256), jnp.bfloat16)
    pad_p[...] = jnp.zeros_like(pad_p)
    for k in range(4):
        for slot in range(REACH):
            lat[k, slot, 0:EDGE, :] = jnp.zeros((EDGE, 128), jnp.float32)
            lat[k, slot, EDGE + rows :, :] = jnp.zeros((EDGE, 128), jnp.float32)
        for t in range(3):
            feat[k, t, 0:EDGE, :] = jnp.zeros((EDGE, 256), jnp.float32)
            feat[k, t, EDGE + rows :, :] = jnp.zeros((EDGE, 256), jnp.float32)

    loads[0].wait()
    values = hid[...].astype(jnp.float32)
    width = values.shape[-1]
    mean = jnp.sum(values, axis=-1, keepdims=True) * (1.0 / width)
    centred = values - mean
    var = jnp.sum(centred * centred, axis=-1, keepdims=True) * (1.0 / width)
    normed = centred * lax.rsqrt(var + 1e-06)
    loads[1].wait()
    modulated = (normed * (1.0 + mod[1:2, :]) + mod[0:1, :]).astype(jnp.bfloat16)
    loads[2].wait()
    for copy in [load_cin] + load_up:
        copy.start()
    patches = lax.dot_general(
        modulated, proj[...], (((1,), (1,)), ((), ())), preferred_element_type=jnp.float32
    )
    pad_p[0:n_tile, 0:64] = patches.astype(jnp.bfloat16).astype(jnp.float32)

    padded = pad_p[...]
    height = padded.shape[0]
    lanes = lax.broadcasted_iota(jnp.int32, padded.shape, 1)
    for i in range(2):
        own = padded if i == 0 else pltpu.roll(padded, 96, 1)
        own = jnp.where(lanes < 32, own, 0.0)
        window = (
            pltpu.roll(own, 1, 0)
            + pltpu.roll(own, 32, 1)
            + pltpu.roll(pltpu.roll(own, height - 1, 0), 64, 1)
        )
        for column in range(n_tile):
            outbox[column, i : i + 1, :] = window[column : column + 1, :]

    own_copy = pltpu.make_async_copy(outbox.at[tile], inbox.at[0, tile], own_sem)
    own_copy.start()
    pl.semaphore_wait(barrier, (after - frame) * n_tile - 1)

    for d in range(REACH):

        @pl.when(frame + d < n_tm)
        def _(d=d):
            def send(step, _):
                column = lax.rem(tile + step, n_tile)
                pltpu.make_async_remote_copy(
                    src_ref=outbox.at[column],
                    dst_ref=inbox.at[d, tile],
                    send_sem=send_sem.at[d],
                    recv_sem=recv_sem.at[d],
                    device_id={"tile": column, "tm": frame + d},
                    device_id_type=MESH,
                ).start()
                return 0

            lax.fori_loop(1 if d == 0 else 0, n_tile, send, 0)

    own_copy.wait()
    for d in range(REACH):
        count = n_tile - 1 if d == 0 else n_tile

        @pl.when(frame - d >= 0)
        def _(d=d, count=count):
            arrived = inbox.at[d, pl.ds(0, count)]
            pltpu.make_async_copy(arrived, arrived, recv_sem.at[d]).wait()

    for slot in range(REACH):
        distance = jnp.minimum(REACH - 1 - slot, frame)
        for r in range(n_tile):
            lat[0, slot, EDGE + 2 * r : EDGE + 2 * r + 2, :] = inbox[distance, r]
        field = lat[0, slot, EDGE : EDGE + rows, :]
        for k in range(1, 4):
            lat[k, slot, EDGE : EDGE + rows, :] = pltpu.roll(field, 128 - 16 * k, 1)

    load_cin.wait()
    taps = []
    for a in range(3):
        for b in range(3):
            start = EDGE - 1 + b
            taps.append(
                jnp.concatenate(
                    [
                        lat[k, t + a, start : start + rows, :]
                        for k in range(4)
                        for t in range(3)
                    ],
                    axis=0,
                ).astype(jnp.bfloat16)
            )
    summed = jnp.dot(
        jnp.concatenate(taps, axis=1),
        cin[...].reshape(9 * 128, 256),
        preferred_element_type=jnp.float32,
    )
    features = (summed / (1.0 + jnp.exp(-summed))).astype(jnp.bfloat16).astype(jnp.float32)
    for k in range(4):
        column = 2 * tile - 1 + k
        inside = jnp.logical_and(column >= 0, column < 2 * n_tile)
        for t in range(3):
            block = features[(3 * k + t) * rows : (3 * k + t + 1) * rows]
            if k in (0, 3):
                block = jnp.where(inside, block, 0.0)
            feat[k, t, EDGE : EDGE + rows, :] = block

    for tap_y in range(3):
        for t in range(3):
            for k in range(4):
                pairs[tap_y, t, k] = jnp.concatenate(
                    [
                        feat[k, t, EDGE + (p + tap_y - 1) // 2 : EDGE + (p + tap_y - 1) // 2 + rows, :]
                        for p in range(2)
                    ],
                    axis=0,
                ).astype(jnp.bfloat16)

    total = None
    for t in range(3):
        load_up[t].wait()
        left = jnp.concatenate(
            [
                jnp.concatenate(
                    [pairs[tap_y, t, (x + tap_x - 1) // 2 + 1] for x in range(4)], axis=0
                )
                for tap_y in range(3)
                for tap_x in range(3)
            ],
            axis=1,
        )
        right = upw[9 * t : 9 * t + 9].reshape(9 * 256, 256)
        part = jnp.dot(left, right, preferred_element_type=jnp.float32)
        total = part if total is None else total + part

    for x in range(4):
        for p in range(2):
            at = (2 * x + p) * rows
            for half in range(2):
                joined[half, pl.ds(4 * p + x, rows, stride=8), :] = total[
                    at : at + rows, 128 * half : 128 * (half + 1)
                ]
    for row in range(2 * rows):
        for half in range(2):
            out_ref[0, row, :, 128 * half : 128 * (half + 1)] = joined[
                half, 4 * row : 4 * row + 4, :
            ].astype(jnp.bfloat16)

    for d in range(REACH):
        count = n_tile - 1 if d == 0 else n_tile

        @pl.when(frame + d < n_tm)
        def _(d=d, count=count):
            left = outbox.at[pl.ds(0, count)]
            pltpu.make_async_copy(left, left, send_sem.at[d]).wait()


def on_device(n_tile, n_tm, hidden, modulation, proj_weight, conv_in_weight, up_weight):
    frames_dev, tokens, width = hidden.shape
    lat_ch, channels = conv_in_weight.shape[3:]
    assert frames_dev == 1 and tokens == n_tile and lat_ch == 16 and channels == 256
    rows = 2 * n_tile
    field = rows + 2 * EDGE
    hbm = pl.BlockSpec(memory_space=pltpu.HBM)
    return pl.pallas_call(
        functools.partial(fused_kernel, n_tile, n_tm),
        out_shape=pltpu.VMEM((1, 2 * rows, 4, channels), jnp.bfloat16),
        in_specs=[hbm] * 5,
        out_specs=pl.BlockSpec(memory_space=pltpu.VMEM),
        scratch_shapes=[
            pltpu.VMEM((tokens, width), jnp.bfloat16),
            pltpu.VMEM((2, width), jnp.float32),
            pltpu.VMEM((4 * lat_ch, width), jnp.bfloat16),
            pltpu.VMEM((9, 128, channels), jnp.bfloat16),
            pltpu.VMEM((27, channels, channels), jnp.bfloat16),
            pltpu.VMEM(((tokens // 8 + 1) * 8, 128), jnp.float32),
            pltpu.VMEM((n_tile, 2, 128), jnp.float32),
            pltpu.VMEM((REACH, n_tile, 2, 128), jnp.float32),
            pltpu.VMEM((4, REACH, field, 128), jnp.float32),
            pltpu.VMEM((4, 3, field, channels), jnp.float32),
            pltpu.VMEM((3, 3, 4, 2 * rows, channels), jnp.bfloat16),
            pltpu.VMEM((2, 8 * rows, 128), jnp.float32),
            pltpu.SemaphoreType.DMA((4,)),
            pltpu.SemaphoreType.DMA((UP_CHUNKS,)),
            pltpu.SemaphoreType.DMA((REACH,)),
            pltpu.SemaphoreType.DMA((REACH,)),
            pltpu.SemaphoreType.DMA,
        ],
        compiler_params=pltpu.CompilerParams(
            collective_id=0, has_side_effects=True
        ),
    )(
        hidden,
        modulation,
        proj_weight.T,
        conv_in_weight.reshape(9, 48, channels),
        up_weight.reshape(27, channels, channels),
    )


def solution(mesh):
    in_specs = (P(("groups", "tm"), "tile", None), P("groups", None), P(), P(), P())
    out_specs = P(("groups", "tm"), None, "tile", None)
    body = functools.partial(on_device, mesh.shape["tile"], mesh.shape["tm"])
    return jax.shard_map(
        body, mesh=mesh, in_specs=in_specs, out_specs=out_specs, check_vma=False
    )
```

```python
import functools

import jax
import jax.numpy as jnp
from jax import lax
from jax.experimental import pallas as pl
from jax.experimental.pallas import tpu as pltpu
from jax.sharding import PartitionSpec as P

REACH = 5
EDGE = 8
UP_CHUNKS = 3
MESH = pl.DeviceIdType.MESH


def fused_kernel(
    n_tile,
    n_tm,
    hidden_hbm,
    mod_hbm,
    proj_hbm,
    cin_hbm,
    up_hbm,
    out_ref,
    hid,
    mod,
    proj,
    cin,
    upw,
    pad_p,
    outbox,
    inbox,
    lat,
    feat,
    pairs,
    joined,
    load_sem,
    up_sem,
    send_sem,
    recv_sem,
    own_sem,
):
    tile = lax.axis_index("tile")
    frame = lax.axis_index("tm")
    rows = 2 * n_tile
    first = jnp.maximum(frame - (REACH - 1), 0)
    after = jnp.minimum(frame + REACH, n_tm)

    barrier = pltpu.get_barrier_semaphore()

    def greet_frame(source, _):
        def greet(column, _):
            @pl.when(jnp.logical_or(source != frame, column != tile))
            def _():
                pl.semaphore_signal(
                    barrier,
                    inc=1,
                    device_id={"tile": column, "tm": source},
                    device_id_type=MESH,
                )

            return 0

        return lax.fori_loop(0, n_tile, greet, 0)

    lax.fori_loop(first, frame + 1, greet_frame, 0)

    loads = [
        pltpu.make_async_copy(hidden_hbm.at[0], hid, load_sem.at[0]),
        pltpu.make_async_copy(mod_hbm, mod, load_sem.at[1]),
        pltpu.make_async_copy(proj_hbm, proj, load_sem.at[2]),
    ]
    load_cin = pltpu.make_async_copy(cin_hbm, cin.at[:, pl.ds(0, 48), :], load_sem.at[3])
    per_chunk = 27 // UP_CHUNKS
    load_up = [
        pltpu.make_async_copy(
            up_hbm.at[pl.ds(n * per_chunk, per_chunk)],
            upw.at[pl.ds(n * per_chunk, per_chunk)],
            up_sem.at[n],
        )
        for n in range(UP_CHUNKS)
    ]
    for copy in loads:
        copy.start()

    cin[:, 48:, :] = jnp.zeros((9, 80, 256), jnp.bfloat16)
    pad_p[...] = jnp.zeros_like(pad_p)
    for k in range(4):
        for slot in range(REACH):
            lat[k, slot, 0:EDGE, :] = jnp.zeros((EDGE, 128), jnp.float32)
            lat[k, slot, EDGE + rows :, :] = jnp.zeros((EDGE, 128), jnp.float32)
        for t in range(3):
            feat[k, t, 0:EDGE, :] = jnp.zeros((EDGE, 256), jnp.float32)
            feat[k, t, EDGE + rows :, :] = jnp.zeros((EDGE, 256), jnp.float32)

    loads[0].wait()
    values = hid[...].astype(jnp.float32)
    width = values.shape[-1]
    mean = jnp.sum(values, axis=-1, keepdims=True) * (1.0 / width)
    centred = values - mean
    var = jnp.sum(centred * centred, axis=-1, keepdims=True) * (1.0 / width)
    normed = centred * lax.rsqrt(var + 1e-06)
    loads[1].wait()
    modulated = (normed * (1.0 + mod[1:2, :]) + mod[0:1, :]).astype(jnp.bfloat16)
    loads[2].wait()
    for copy in [load_cin] + load_up:
        copy.start()
    patches = lax.dot_general(
        modulated, proj[...], (((1,), (1,)), ((), ())), preferred_element_type=jnp.float32
    )
    pad_p[0:n_tile, 0:64] = patches.astype(jnp.bfloat16).astype(jnp.float32)

    padded = pad_p[...]
    height = padded.shape[0]
    lanes = lax.broadcasted_iota(jnp.int32, padded.shape, 1)
    for i in range(2):
        own = padded if i == 0 else pltpu.roll(padded, 96, 1)
        own = jnp.where(lanes < 32, own, 0.0)
        window = (
            pltpu.roll(own, 1, 0)
            + pltpu.roll(own, 32, 1)
            + pltpu.roll(pltpu.roll(own, height - 1, 0), 64, 1)
        )
        for column in range(n_tile):
            outbox[column, i : i + 1, :] = window[column : column + 1, :]

    own_copy = pltpu.make_async_copy(outbox.at[tile], inbox.at[0, tile], own_sem)
    own_copy.start()
    pl.semaphore_wait(barrier, (after - frame) * n_tile - 1)

    for d in range(REACH):

        @pl.when(frame + d < n_tm)
        def _(d=d):
            def send(step, _):
                column = lax.rem(tile + step, n_tile)
                pltpu.make_async_remote_copy(
                    src_ref=outbox.at[column],
                    dst_ref=inbox.at[d, tile],
                    send_sem=send_sem.at[d],
                    recv_sem=recv_sem.at[d],
                    device_id={"tile": column, "tm": frame + d},
                    device_id_type=MESH,
                ).start()
                return 0

            lax.fori_loop(1 if d == 0 else 0, n_tile, send, 0)

    own_copy.wait()
    for d in range(REACH):
        count = n_tile - 1 if d == 0 else n_tile

        @pl.when(frame - d >= 0)
        def _(d=d, count=count):
            arrived = inbox.at[d, pl.ds(0, count)]
            pltpu.make_async_copy(arrived, arrived, recv_sem.at[d]).wait()

    for slot in range(REACH):
        distance = jnp.minimum(REACH - 1 - slot, frame)
        for r in range(n_tile):
            lat[0, slot, EDGE + 2 * r : EDGE + 2 * r + 2, :] = inbox[distance, r]
        field = lat[0, slot, EDGE : EDGE + rows, :]
        for k in range(1, 4):
            lat[k, slot, EDGE : EDGE + rows, :] = pltpu.roll(field, 128 - 16 * k, 1)

    load_cin.wait()
    taps = []
    for a in range(3):
        for b in range(3):
            start = EDGE - 1 + b
            taps.append(
                jnp.concatenate(
                    [
                        lat[k, t + a, start : start + rows, :]
                        for k in range(4)
                        for t in range(3)
                    ],
                    axis=0,
                ).astype(jnp.bfloat16)
            )
    summed = jnp.dot(
        jnp.concatenate(taps, axis=1),
        cin[...].reshape(9 * 128, 256),
        preferred_element_type=jnp.float32,
    )
    features = (summed / (1.0 + jnp.exp(-summed))).astype(jnp.bfloat16).astype(jnp.float32)
    for k in range(4):
        column = 2 * tile - 1 + k
        inside = jnp.logical_and(column >= 0, column < 2 * n_tile)
        for t in range(3):
            block = features[(3 * k + t) * rows : (3 * k + t + 1) * rows]
            if k in (0, 3):
                block = jnp.where(inside, block, 0.0)
            feat[k, t, EDGE : EDGE + rows, :] = block

    for tap_y in range(3):
        for t in range(3):
            for k in range(4):
                pairs[tap_y, t, k] = jnp.concatenate(
                    [
                        feat[k, t, EDGE + (p + tap_y - 1) // 2 : EDGE + (p + tap_y - 1) // 2 + rows, :]
                        for p in range(2)
                    ],
                    axis=0,
                ).astype(jnp.bfloat16)

    for t in range(3):
        load_up[t].wait()
    left = jnp.concatenate(
        [
            jnp.concatenate(
                [pairs[tap_y, t, (x + tap_x - 1) // 2 + 1] for x in range(4)], axis=0
            )
            for t in range(3)
            for tap_y in range(3)
            for tap_x in range(3)
        ],
        axis=1,
    )
    total = jnp.dot(
        left, upw[...].reshape(27 * 256, 256), preferred_element_type=jnp.float32
    )

    for x in range(4):
        for p in range(2):
            at = (2 * x + p) * rows
            for half in range(2):
                joined[half, pl.ds(4 * p + x, rows, stride=8), :] = total[
                    at : at + rows, 128 * half : 128 * (half + 1)
                ]
    for row in range(2 * rows):
        for half in range(2):
            out_ref[0, row, :, 128 * half : 128 * (half + 1)] = joined[
                half, 4 * row : 4 * row + 4, :
            ].astype(jnp.bfloat16)

    for d in range(REACH):
        count = n_tile - 1 if d == 0 else n_tile

        @pl.when(frame + d < n_tm)
        def _(d=d, count=count):
            left = outbox.at[pl.ds(0, count)]
            pltpu.make_async_copy(left, left, send_sem.at[d]).wait()


def on_device(n_tile, n_tm, hidden, modulation, proj_weight, conv_in_weight, up_weight):
    frames_dev, tokens, width = hidden.shape
    lat_ch, channels = conv_in_weight.shape[3:]
    assert frames_dev == 1 and tokens == n_tile and lat_ch == 16 and channels == 256
    rows = 2 * n_tile
    field = rows + 2 * EDGE
    hbm = pl.BlockSpec(memory_space=pltpu.HBM)
    return pl.pallas_call(
        functools.partial(fused_kernel, n_tile, n_tm),
        out_shape=pltpu.VMEM((1, 2 * rows, 4, channels), jnp.bfloat16),
        in_specs=[hbm] * 5,
        out_specs=pl.BlockSpec(memory_space=pltpu.VMEM),
        scratch_shapes=[
            pltpu.VMEM((tokens, width), jnp.bfloat16),
            pltpu.VMEM((2, width), jnp.float32),
            pltpu.VMEM((4 * lat_ch, width), jnp.bfloat16),
            pltpu.VMEM((9, 128, channels), jnp.bfloat16),
            pltpu.VMEM((27, channels, channels), jnp.bfloat16),
            pltpu.VMEM(((tokens // 8 + 1) * 8, 128), jnp.float32),
            pltpu.VMEM((n_tile, 2, 128), jnp.float32),
            pltpu.VMEM((REACH, n_tile, 2, 128), jnp.float32),
            pltpu.VMEM((4, REACH, field, 128), jnp.float32),
            pltpu.VMEM((4, 3, field, channels), jnp.float32),
            pltpu.VMEM((3, 3, 4, 2 * rows, channels), jnp.bfloat16),
            pltpu.VMEM((2, 8 * rows, 128), jnp.float32),
            pltpu.SemaphoreType.DMA((4,)),
            pltpu.SemaphoreType.DMA((UP_CHUNKS,)),
            pltpu.SemaphoreType.DMA((REACH,)),
            pltpu.SemaphoreType.DMA((REACH,)),
            pltpu.SemaphoreType.DMA,
        ],
        compiler_params=pltpu.CompilerParams(
            collective_id=0, has_side_effects=True
        ),
    )(
        hidden,
        modulation,
        proj_weight.T,
        conv_in_weight.reshape(9, 48, channels),
        up_weight.reshape(27, channels, channels),
    )


def solution(mesh):
    in_specs = (P(("groups", "tm"), "tile", None), P("groups", None), P(), P(), P())
    out_specs = P(("groups", "tm"), None, "tile", None)
    body = functools.partial(on_device, mesh.shape["tile"], mesh.shape["tm"])
    return jax.shard_map(
        body, mesh=mesh, in_specs=in_specs, out_specs=out_specs, check_vma=False
    )
```
